512 devices in a mesh: dp: 16 (over z_hi, y), row: 8 (over x, core), col: 4 (over z_lo).
Axes of the slice: x: 4, y: 8, z: 8 (z_hi: 2, z_lo: 4; z = z_hi * 4 + z_lo), core: 2. Of those that a mesh axis runs over, the one named last changes fastest.
Arguments:
- inputs: bfloat16 [16, 512, 4, 1536], P('dp', 'col', None, 'row'), may hold values from -12 to 12
- gain: bfloat16 [4, 1536], P(None, 'row'), may hold values from 0.099609375 to 1.8984375
- weight: bfloat16 [6144, 6144], P('col', 'row'), may hold values from -0.078125 to 0.078125
- cotangent: bfloat16 [16, 512, 6144], P('dp', 'col', 'row'), may hold values from -3 to 3
Outputs:
- outputs: bfloat16 [16, 512, 6144], P('dp', 'col', 'row')
- input_grad: bfloat16 [16, 512, 4, 1536], P('dp', 'col', None, 'row')
- gain_grad: float32 [4, 1536], P(None, 'row')
- weight_grad: float32 [4, 1536, 6144], P('col', 'dp', 'row')
The draws below stay inside these ranges and needn't reach their ends.
All inputs are finite; a program needn't handle non-finite values.
Results may differ from the reference program's by a relative error of at most 0.014.
Values may be sent and summed in bfloat16 or wider, within the bound.
A program may use at most 64 MiB of HBM per device.

```python
import jax
import jax.numpy as jnp
from jax import lax

D = 6144
E = 6144
TOKENS = 512
GROUPS = 16
N_ROW = 8
N_COL = 4


def draw_inputs(key, part):
    first_key, second_key, third_key = jax.random.split(key, 3)
    shape = (GROUPS, TOKENS, N_COL, D // N_COL)
    row_scale = jnp.exp(jax.random.uniform(second_key, (GROUPS, TOKENS, 1, 1), jnp.float32, jnp.log(0.1), 0.0))
    col_scale = jnp.exp(jax.random.uniform(third_key, (1, 1, N_COL, D // N_COL), jnp.float32, jnp.log(0.3), jnp.log(3.0)))
    rough = jnp.clip(jax.random.normal(first_key, shape, jnp.float32), -4.0, 4.0)
    result = rough * col_scale * row_scale
    return result.astype(jnp.bfloat16)


def block_levels(stream_key, dims, shards, smallest, high):
    level, own = 1.0, jax.random.fold_in(stream_key, 6)
    for position, shards_of in shards:
        heights = jnp.exp(jax.random.uniform(jax.random.fold_in(own, position), (shards_of,), jnp.float32, smallest / len(shards), high / len(shards)))
        level = level * jnp.repeat(heights, dims[position] // shards_of).reshape([-1 if axis == position else 1 for axis in range(len(dims))])
    return level


def centred(key, shape, scale, limit, cuts=(), held_as=jnp.bfloat16):
    entries = jax.random.normal(key, shape, jnp.float32) * scale
    if len(cuts) > 0:
        entries = block_levels(key, shape, cuts, -0.22, 0.18) * entries
    return jnp.clip(entries, min=-limit, max=limit).astype(held_as)


def setup_inputs(seed: int = 0) -> dict:
    arg_keys = jax.random.split(jax.random.key(seed), 5)
    return {
        "inputs": draw_inputs(jax.random.fold_in(arg_keys[4], 71), 0),
        "gain": jnp.clip(1.0 + 0.18 * jax.random.normal(arg_keys[1], (N_COL, D // N_COL), jnp.float32), 0.099609375, 1.8984375).astype(jnp.bfloat16),
        "weight": centred(arg_keys[2], (D, E), D ** -0.5, 0.078125, ((0, 4), (1, 8))),
        "cotangent": centred(arg_keys[3], (GROUPS, TOKENS, E), 0.5, 3.0, ((0, 16), (1, 4), (2, 8))),
    }


EPS = 1e-05

def reference(inputs, gain, weight, cotangent):
    values = inputs.reshape(GROUPS * TOKENS, D).astype(jnp.float32)
    scale = gain.reshape(D).astype(jnp.float32)
    mean = lax.optimization_barrier(jnp.mean(values, axis=1, keepdims=True))
    variance = lax.optimization_barrier(jnp.mean(values * values, axis=1, keepdims=True)) - mean * mean
    inv_std = lax.rsqrt(variance + EPS)
    normed = (values - mean) * inv_std
    hidden = (normed * scale).astype(jnp.bfloat16)
    outputs = jnp.dot(hidden, weight, preferred_element_type=jnp.float32).astype(jnp.bfloat16)
    cot_rows = cotangent.reshape(GROUPS * TOKENS, E)
    block_width = E // N_ROW
    back = jnp.zeros((GROUPS * TOKENS, D), jnp.float32)
    for block in range(N_ROW):
        lower = block * block_width
        product = jnp.dot(cot_rows[:, lower:lower + block_width], weight[:, lower:lower + block_width].T, preferred_element_type=jnp.float32)
        rounded = lax.optimization_barrier(product.astype(jnp.bfloat16))
        back = back + rounded.astype(jnp.float32)
    scaled = back * scale
    first = lax.optimization_barrier(jnp.mean(scaled, axis=1, keepdims=True))
    second = lax.optimization_barrier(jnp.mean(scaled * normed, axis=1, keepdims=True))
    input_grad = (inv_std * (scaled - first - normed * second)).astype(jnp.bfloat16).reshape(GROUPS, TOKENS, N_COL, D // N_COL)
    gain_grad = (lax.optimization_barrier(jnp.sum(back * normed, axis=0)) / GROUPS).reshape(N_COL, D // N_COL)
    hidden_groups = hidden.reshape(GROUPS, TOKENS, D)
    grad_sum = jnp.zeros((D, E), jnp.float32)
    for group in range(GROUPS):
        product = jnp.dot(hidden_groups[group].T, cotangent[group], preferred_element_type=jnp.float32)
        rounded = lax.optimization_barrier(product.astype(jnp.bfloat16))
        grad_sum = grad_sum + rounded.astype(jnp.float32)
    weight_grad = (grad_sum / GROUPS).reshape(N_COL, D // N_COL, E)
    outputs = outputs.reshape(GROUPS, TOKENS, E)
    return (outputs, input_grad, gain_grad, weight_grad)
```

```python
import functools

import jax
import jax.numpy as jnp
from jax import lax
from jax.experimental import pallas as pl
from jax.experimental.pallas import tpu as pltpu
from jax.sharding import PartitionSpec as P

EPS = 1e-05
F32 = jnp.float32
BF16 = jnp.bfloat16
YS = 8
XS = 4
COPIES = 96


def al(value, to):
    return pl.multiple_of(value, to)


def kernel(
    x_ref, g_ref, w_ref, cot_ref,
    out_ref, ig_ref, gg_ref, wg_ref,
    stat, statr, normed, hid, gcol, panel, cotp, bsend, sibr,
    f1s, f1r, f2s, f2r, gs, bl, hst, hstr, osend, orecv, ofull,
    prod, rs, rr, zs, zr, gcb, gyb, gzs, gzr, ssem, rsem,
):
    blocks, share, tokens = x_ref.shape
    wide = cot_ref.shape[1]
    n_row, n_col, n_dp = lax.axis_size("row"), lax.axis_size("col"), lax.axis_size("dp")
    part = n_row * share
    width = n_row * blocks * share
    piece = part // n_dp
    half = wide // 2
    pair = 2 * tokens

    dp, row, col = lax.axis_index("dp"), lax.axis_index("row"), lax.axis_index("col")
    zh, y = dp // YS, dp % YS
    x, core = row // 2, row % 2
    cols = [col, col + 1 - 2 * (col % 2), (col + 2) % n_col, n_col - 1 - col]

    def at_row(r):
        return {"row": r}

    def at_x(step):
        return {"row": ((x + step + XS) % XS) * 2 + core}

    def at_col(c):
        return {"col": c}

    def at_y(step):
        return {"dp": zh * YS + (y + step + YS) % YS}

    sibling = {"row": x * 2 + 1 - core}
    partner = {"dp": (dp + YS) % n_dp}

    started = []

    def send(src, dst, device):
        index = len(started)
        copy = pltpu.make_async_remote_copy(
            src_ref=src,
            dst_ref=dst,
            send_sem=ssem.at[index],
            recv_sem=rsem.at[index],
            device_id=device,
            device_id_type=pl.DeviceIdType.MESH,
        )
        copy.start()
        started.append(copy)
        return copy

    barrier = pltpu.get_barrier_semaphore()
    peers = [at_row((row + k) % n_row) for k in range(1, n_row)]
    peers += [at_col(cols[k]) for k in range(1, n_col)]
    peers += [at_y(k) for k in range(1, YS)]
    peers += [partner]
    for peer in peers:
        pl.semaphore_signal(barrier, inc=1, device_id=peer, device_id_type=pl.DeviceIdType.MESH)

    values = x_ref[...].astype(F32)
    stat[0:1, :] = jnp.sum(values, axis=(0, 1)).reshape(1, tokens)
    stat[1:2, :] = jnp.sum(values * values, axis=(0, 1)).reshape(1, tokens)
    gcol[...] = jnp.transpose(jnp.broadcast_to(g_ref[...], (tokens, blocks * share)))
    cotp[pl.ds(al(col * tokens, tokens), tokens), :] = cot_ref[...]
    pl.semaphore_wait(barrier, len(peers))

    own_rows = pl.ds(al(col * tokens, tokens), tokens)
    stats = [send(stat, statr.at[k], at_row((row + k) % n_row)) for k in range(1, n_row)]
    cots = {1: send(cot_ref, cotp.at[own_rows, :], at_col(cols[1]))}

    total = stat[...]
    for k in range(1, n_row):
        stats[k - 1].wait_recv()
        total = total + statr[k]
    mean = total[0:1, :] / width
    variance = total[1:2, :] / width - mean * mean
    inv_std = lax.rsqrt(variance + EPS)
    flat = x_ref[...].astype(F32).reshape(blocks * share, tokens)
    norm = (flat - mean) * inv_std
    normed[...] = norm
    hid[...] = (norm * gcol[...]).astype(BF16).reshape(blocks, share, tokens)

    mine = pl.ds(al(row * share, share), share)
    own_lanes = pl.ds(al(col * tokens, tokens), tokens)
    moves = {k: send(hid.at[cols[k]], panel.at[mine, own_lanes], at_col(cols[k])) for k in (1, 3, 2)}
    panel[mine, own_lanes] = hid[col]
    for k in (3, 2):
        cots[k] = send(cot_ref, cotp.at[own_rows, :], at_col(cols[k]))

    def back_pair(p):
        lanes = pl.ds(al(p * pair, pair), pair)
        rhs_rows = pl.ds(al(p * pair, pair), pair)
        step = part // 2

        @pl.loop(0, 2)
        def _(i):
            rows = pl.ds(al(i * step, step), step)
            bsend[rows, lanes] = lax.dot_general(
                w_ref[rows, :], cotp[rhs_rows, :], (((1,), (1,)), ((), ())), preferred_element_type=F32
            ).astype(BF16)

        return [
            send(
                bsend.at[pl.ds(al((2 * xd + 1 - core) * share, share), share), lanes],
                sibr.at[xd, :, lanes],
                sibling,
            )
            for xd in range(XS)
        ]

    cots[1].wait_recv()
    sibs = back_pair(col // 2)

    for k in (1, 3, 2):
        moves[k].wait_recv()

    def block_of(step):
        return pl.ds(al((((x + step + XS) % XS) * 2 + core) * share, share), share)

    right = send(panel.at[mine, :], panel.at[mine, :], at_x(1))
    left = send(panel.at[mine, :], panel.at[mine, :], at_x(-1))
    gathers = [send(panel.at[mine, :], panel.at[mine, :], sibling)]
    low, high = pl.ds(0, pair), pl.ds(pair, pair)
    right.wait_recv()
    relay_right = send(panel.at[block_of(-1), low], panel.at[block_of(-1), low], at_x(1))
    gathers.append(send(panel.at[block_of(-1), :], panel.at[block_of(-1), :], sibling))
    left.wait_recv()
    relay_left = send(panel.at[block_of(1), high], panel.at[block_of(1), high], at_x(-1))
    gathers.append(send(panel.at[block_of(1), :], panel.at[block_of(1), :], sibling))
    relay_right.wait_recv()
    relay_left.wait_recv()
    gathers.append(send(panel.at[block_of(2), :], panel.at[block_of(2), :], sibling))
    for k in (3, 2):
        cots[k].wait_recv()
    for copy in gathers:
        copy.wait_recv()

    def grad_rows(targets):
        return jnp.concatenate(
            [panel[pl.ds(al((sub * YS + t) * piece, piece), piece), :] for sub, t in targets], axis=0
        )

    def product(targets):
        prod[0 : len(targets) * piece, :] = jnp.dot(
            grad_rows(targets), cotp[...], preferred_element_type=F32
        )

    ring = {}
    sides = (1, -1)

    def ring_start():
        opposite = (y + YS // 2) % YS
        product([(0, opposite), (1, opposite)])
        for h in range(2):
            for d in range(2):
                rs[d, h, 0, d] = prod[d * piece : (d + 1) * piece, h * half : (h + 1) * half].astype(BF16)
        for h in range(2):
            for d in range(2):
                ring[d, h, 0] = send(rs.at[d, h, 0, d], rr.at[d, h, 0, d], at_y(sides[d]))

    def ring_product(s):
        forward, backward = (y + YS // 2 - s) % YS, (y + YS // 2 + s) % YS
        product([(0, forward), (1, forward), (0, backward), (1, backward)])

    def ring_step(s):
        for h in range(2):
            for d in range(2):
                ring[d, h, s - 1].wait_recv()
                for sub in range(2):
                    at = (2 * d + sub) * piece
                    value = prod[at : at + piece, h * half : (h + 1) * half]
                    if s > 1 or sub == d:
                        value = value + rr[d, h, s - 1, sub].astype(F32)
                    rs[d, h, s, sub] = value.astype(BF16)
                ring[d, h, s] = send(rs.at[d, h, s], rr.at[d, h, s], at_y(sides[d]))

    last = YS // 2 - 1
    across = []

    def ring_end():
        for h in range(2):
            lanes = slice(h * half, (h + 1) * half)
            for d in range(2):
                ring[d, h, last].wait_recv()
            there = prod[piece : 2 * piece, lanes]
            there = there + rr[0, h, last, 1 - zh].astype(F32) + rr[1, h, last, 1 - zh].astype(F32)
            zs[h] = there.astype(BF16)
            across.append(send(zs.at[h], zr.at[h], partner))
            here = prod[0:piece, lanes]
            wg_ref[:, lanes] = here + rr[0, h, last, zh].astype(F32) + rr[1, h, last, zh].astype(F32)

    def out_pair(p):
        lhs = jnp.transpose(panel[:, pl.ds(al(p * pair, pair), pair)])
        ofull[...] = jnp.dot(lhs, w_ref[...], preferred_element_type=F32)
        osend[2 * p] = ofull[0:tokens, :].astype(BF16)
        osend[2 * p + 1] = ofull[tokens:pair, :].astype(BF16)

    def partial(xd):
        rows = pl.ds(al((2 * xd + core) * share, share), share)
        return bsend[rows, :].astype(F32) + sibr[xd].astype(F32)

    ring_start()
    ring_product(1)
    sibs += back_pair(1 - col // 2)
    ring_step(1)
    ring_product(2)
    out_pair(1 - col // 2)
    outs = {k: send(osend.at[cols[k]], orecv.at[k], at_col(cols[k])) for k in (3, 2)}
    ring_step(2)
    ring_product(3)
    for copy in sibs:
        copy.wait_recv()
    far = partial((x + 2) % XS)
    f1s[0] = far[:, 0:pair].astype(BF16)
    f1s[1] = far[:, pair : 2 * pair].astype(BF16)
    first_hop = [send(f1s.at[d], f1r.at[d], at_x(sides[d])) for d in range(2)]
    ring_step(3)
    product([(zh, y), (1 - zh, y)])
    out_pair(col // 2)
    outs[1] = send(osend.at[cols[1]], orecv.at[1], at_col(cols[1]))
    second_hop = []
    for d in range(2):
        near = partial((x + sides[d] + XS) % XS)
        first_hop[d].wait_recv()
        for i in range(2):
            value = near[:, i * pair : (i + 1) * pair]
            if i == d:
                value = value + f1r[d].astype(F32)
            f2s[d, :, i * pair : (i + 1) * pair] = value.astype(BF16)
        second_hop.append(send(f2s.at[d], f2r.at[d], at_x(sides[d])))
    ring_end()

    back = partial(x)
    for d in range(2):
        second_hop[d].wait_recv()
        back = back + f2r[d].astype(F32)
    for c in range(blocks):
        gs[c] = back[:, c * tokens : (c + 1) * tokens].astype(BF16)
    turns = [send(gs.at[cols[k]], bl.at[col], at_col(cols[k])) for k in (1, 2, 3)]
    bl[col] = gs[col]
    result = ofull[pl.ds(al((col % 2) * tokens, tokens), tokens), :]
    for k in (3, 2, 1):
        outs[k].wait_recv()
        result = result + orecv[k].astype(F32)
    out_ref[...] = result.astype(BF16)

    for copy in turns:
        copy.wait_recv()
    back = bl[...].astype(F32).reshape(blocks * share, tokens)
    scaled = back * gcol[...]
    hst[0:1, :] = jnp.sum(scaled, axis=0, keepdims=True)
    hst[1:2, :] = jnp.sum(scaled * normed[...], axis=0, keepdims=True)
    means = [send(hst, hstr.at[k], at_row((row + k) % n_row)) for k in range(1, n_row)]
    gcb[col] = jnp.sum(jnp.transpose(back * normed[...]), axis=0, keepdims=True)
    gain_cols = [send(gcb.at[col], gcb.at[col], at_col(cols[k])) for k in range(1, n_col)]

    sums = hst[...]
    for k in range(1, n_row):
        means[k - 1].wait_recv()
        sums = sums + hstr[k]
    first = sums[0:1, :] / width
    second = sums[1:2, :] / width
    grad = inv_std * (scaled - first - normed[...] * second)
    ig_ref[...] = grad.astype(BF16).reshape(blocks, share, tokens)

    for copy in gain_cols:
        copy.wait_recv()
    gyb[y] = gcb[0] + gcb[1] + gcb[2] + gcb[3]
    gain_ys = [send(gyb.at[y], gyb.at[y], at_y(k)) for k in range(1, YS)]
    for h in range(2):
        across[h].wait_recv()
        lanes = slice(h * half, (h + 1) * half)
        wg_ref[:, lanes] = (wg_ref[:, lanes] + zr[h].astype(F32)) / n_dp
    for copy in gain_ys:
        copy.wait_recv()
    group = gyb[0]
    for i in range(1, YS):
        group = group + gyb[i]
    gzs[...] = group
    gain_z = send(gzs, gzr, partner)
    gain_z.wait_recv()
    gg_ref[...] = (gzs[...] + gzr[...]) / n_dp
    for copy in started:
        copy.wait_send()


def body(inputs, gain, weight, cotangent):
    tokens, blocks, share = inputs.shape[1:]
    part, wide = weight.shape
    n_dp, n_row, n_col = lax.axis_size("dp"), lax.axis_size("row"), lax.axis_size("col")
    piece = part // n_dp
    half = wide // 2
    pair = 2 * tokens
    vmem = pl.BlockSpec(memory_space=pltpu.VMEM)
    outputs, input_grad, gain_grad, weight_grad = pl.pallas_call(
        kernel,
        out_shape=(
            jax.ShapeDtypeStruct((tokens, wide), BF16),
            jax.ShapeDtypeStruct((blocks, share, tokens), BF16),
            jax.ShapeDtypeStruct((1, blocks * share), F32),
            jax.ShapeDtypeStruct((piece, wide), F32),
        ),
        in_specs=[vmem] * 4,
        out_specs=(vmem,) * 4,
        scratch_shapes=[
            pltpu.VMEM((2, tokens), F32),
            pltpu.VMEM((n_row, 2, tokens), F32),
            pltpu.VMEM((blocks * share, tokens), F32),
            pltpu.VMEM((blocks, share, tokens), BF16),
            pltpu.VMEM((blocks * share, tokens), F32),
            pltpu.VMEM((part, n_col * tokens), BF16),
            pltpu.VMEM((n_col * tokens, wide), BF16),
            pltpu.VMEM((part, n_col * tokens), BF16),
            pltpu.VMEM((XS, share, n_col * tokens), BF16),
            pltpu.VMEM((2, share, pair), BF16),
            pltpu.VMEM((2, share, pair), BF16),
            pltpu.VMEM((2, share, 2 * pair), BF16),
            pltpu.VMEM((2, share, 2 * pair), BF16),
            pltpu.VMEM((n_col, share, tokens), BF16),
            pltpu.VMEM((n_col, share, tokens), BF16),
            pltpu.VMEM((2, tokens), F32),
            pltpu.VMEM((n_row, 2, tokens), F32),
            pltpu.VMEM((n_col, tokens, wide), BF16),
            pltpu.VMEM((n_col, tokens, wide), BF16),
            pltpu.VMEM((pair, wide), F32),
            pltpu.VMEM((4 * piece, wide), F32),
            pltpu.VMEM((2, 2, YS // 2, 2, piece, half), BF16),
            pltpu.VMEM((2, 2, YS // 2, 2, piece, half), BF16),
            pltpu.VMEM((2, piece, half), BF16),
            pltpu.VMEM((2, piece, half), BF16),
            pltpu.VMEM((n_col, 1, blocks * share), F32),
            pltpu.VMEM((YS, 1, blocks * share), F32),
            pltpu.VMEM((1, blocks * share), F32),
            pltpu.VMEM((1, blocks * share), F32),
            pltpu.SemaphoreType.DMA((COPIES,)),
            pltpu.SemaphoreType.DMA((COPIES,)),
        ],
        compiler_params=pltpu.CompilerParams(collective_id=0, has_side_effects=True),
    )(
        jnp.transpose(inputs[0], (1, 2, 0)),
        gain.astype(F32).reshape(1, blocks * share),
        weight,
        cotangent[0],
    )
    return (
        outputs[None],
        jnp.transpose(input_grad, (2, 0, 1))[None],
        gain_grad.reshape(blocks, share),
        weight_grad[None],
    )


def solution(mesh):
    return jax.shard_map(
        body,
        mesh=mesh,
        in_specs=(
            P("dp", "col", None, "row"),
            P(None, "row"),
            P("col", "row"),
            P("dp", "col", "row"),
        ),
        out_specs=(
            P("dp", "col", "row"),
            P("dp", "col", None, "row"),
            P(None, "row"),
            P("col", "dp", "row"),
        ),
        check_vma=False,
    )
```

```python
import functools

import jax
import jax.numpy as jnp
from jax import lax
from jax.experimental import pallas as pl
from jax.experimental.pallas import tpu as pltpu
from jax.sharding import PartitionSpec as P

EPS = 1e-05
F32 = jnp.float32
BF16 = jnp.bfloat16
YS = 8
XS = 4
COPIES = 96


def al(value, to):
    return pl.multiple_of(value, to)


def kernel(
    x_ref, g_ref, w_hbm, cot_ref,
    out_ref, ig_ref, gg_ref, wg_ref,
    stat, statr, normed, hid, gcol, panel, cotp, bsend, sibr,
    f1s, f1r, f2s, f2r, gs, bl, hst, hstr, osend, orecv, osum, ofull, w_ref,
    prod, rs, rr, zs, zr, gcb, gyb, gzs, gzr, ssem, rsem, wsem,
):
    blocks, share, tokens = x_ref.shape
    wide = cot_ref.shape[1]
    n_row, n_col, n_dp = lax.axis_size("row"), lax.axis_size("col"), lax.axis_size("dp")
    part = n_row * share
    width = n_row * blocks * share
    piece = part // n_dp
    half = wide // 2
    pair = 2 * tokens

    dp, row, col = lax.axis_index("dp"), lax.axis_index("row"), lax.axis_index("col")
    zh, y = dp // YS, dp % YS
    x, core = row // 2, row % 2
    cols = [col, col + 1 - 2 * (col % 2), (col + 2) % n_col, n_col - 1 - col]

    def at_row(r):
        return {"row": r}

    def at_x(step):
        return {"row": ((x + step + XS) % XS) * 2 + core}

    def at_col(c):
        return {"col": c}

    def at_y(step):
        return {"dp": zh * YS + (y + step + YS) % YS}

    sibling = {"row": x * 2 + 1 - core}
    partner = {"dp": (dp + YS) % n_dp}

    weight_in = pltpu.make_async_copy(w_hbm, w_ref, wsem)
    weight_in.start()
    started = []

    def send(src, dst, device):
        index = len(started)
        copy = pltpu.make_async_remote_copy(
            src_ref=src,
            dst_ref=dst,
            send_sem=ssem.at[index],
            recv_sem=rsem.at[index],
            device_id=device,
            device_id_type=pl.DeviceIdType.MESH,
        )
        copy.start()
        started.append(copy)
        return copy

    barrier = pltpu.get_barrier_semaphore()
    peers = [at_row((row + k) % n_row) for k in range(1, n_row)]
    peers += [at_col(cols[k]) for k in range(1, n_col)]
    peers += [at_y(k) for k in range(1, YS)]
    peers += [partner]
    for peer in peers:
        pl.semaphore_signal(barrier, inc=1, device_id=peer, device_id_type=pl.DeviceIdType.MESH)

    values = x_ref[...].astype(F32)
    stat[0:1, :] = jnp.sum(values, axis=(0, 1)).reshape(1, tokens)
    stat[1:2, :] = jnp.sum(values * values, axis=(0, 1)).reshape(1, tokens)
    cotp[pl.ds(al(col * tokens, tokens), tokens), :] = cot_ref[...]
    pl.semaphore_wait(barrier, len(peers))

    own_rows = pl.ds(al(col * tokens, tokens), tokens)
    stats = [send(stat, statr.at[k], at_row((row + k) % n_row)) for k in range(1, n_row)]
    cots = {k: send(cot_ref, cotp.at[own_rows, :], at_col(cols[k])) for k in (1, 3)}
    gain = g_ref[...].astype(F32)
    for a in range(blocks):
        gcol[a * share : (a + 1) * share, :] = jnp.transpose(
            jnp.broadcast_to(gain[a : a + 1, :], (tokens, share))
        )

    total = stat[...]
    for k in range(1, n_row):
        stats[k - 1].wait_recv()
        total = total + statr[k]
    mean = total[0:1, :] / width
    variance = total[1:2, :] / width - mean * mean
    inv_std = lax.rsqrt(variance + EPS)
    flat = x_ref[...].astype(F32).reshape(blocks * share, tokens)
    norm = (flat - mean) * inv_std
    normed[...] = norm
    hid[...] = (norm * gcol[...]).astype(BF16).reshape(blocks, share, tokens)

    mine = pl.ds(al(row * share, share), share)
    own_lanes = pl.ds(al(col * tokens, tokens), tokens)
    moves = {k: send(hid.at[cols[k]], panel.at[mine, own_lanes], at_col(cols[k])) for k in (1, 3, 2)}
    panel[mine, own_lanes] = hid[col]
    cots[3].wait_recv()
    passed = pl.ds(al(cols[3] * tokens, tokens), tokens)
    cots[2] = send(cotp.at[passed, :], cotp.at[passed, :], at_col(cols[1]))

    def back_pair(p):
        lanes = pl.ds(al(p * pair, pair), pair)
        rhs_rows = pl.ds(al(p * pair, pair), pair)
        step = part // 2

        @pl.loop(0, 2)
        def _(i):
            rows = pl.ds(al(i * step, step), step)
            bsend[rows, lanes] = lax.dot_general(
                w_ref[rows, :], cotp[rhs_rows, :], (((1,), (1,)), ((), ())), preferred_element_type=F32
            ).astype(BF16)

        return [
            send(
                bsend.at[pl.ds(al((2 * xd + 1 - core) * share, share), share), lanes],
                sibr.at[xd, :, lanes],
                sibling,
            )
            for xd in range(XS)
        ]

    cots[1].wait_recv()
    weight_in.wait()
    sibs = back_pair(col // 2)

    for k in (1, 3, 2):
        moves[k].wait_recv()

    def block_of(step):
        return pl.ds(al((((x + step + XS) % XS) * 2 + core) * share, share), share)

    right = send(panel.at[mine, :], panel.at[mine, :], at_x(1))
    left = send(panel.at[mine, :], panel.at[mine, :], at_x(-1))
    gathers = [send(panel.at[mine, :], panel.at[mine, :], sibling)]
    low, high = pl.ds(0, pair), pl.ds(pair, pair)
    right.wait_recv()
    relay_right = send(panel.at[block_of(-1), low], panel.at[block_of(-1), low], at_x(1))
    gathers.append(send(panel.at[block_of(-1), :], panel.at[block_of(-1), :], sibling))
    left.wait_recv()
    relay_left = send(panel.at[block_of(1), high], panel.at[block_of(1), high], at_x(-1))
    gathers.append(send(panel.at[block_of(1), :], panel.at[block_of(1), :], sibling))
    relay_right.wait_recv()
    relay_left.wait_recv()
    gathers.append(send(panel.at[block_of(2), :], panel.at[block_of(2), :], sibling))
    def partial(xd):
        rows = pl.ds(al((2 * xd + core) * share, share), share)
        return bsend[rows, :].astype(F32) + sibr[xd].astype(F32)

    sides = (1, -1)
    cots[2].wait_recv()
    sibs += back_pair(1 - col // 2)
    for copy in sibs:
        copy.wait_recv()
    far = partial((x + 2) % XS)
    f1s[0] = far[:, 0:pair].astype(BF16)
    f1s[1] = far[:, pair : 2 * pair].astype(BF16)
    first_hop = [send(f1s.at[d], f1r.at[d], at_x(sides[d])) for d in range(2)]
    for copy in gathers:
        copy.wait_recv()

    def grad_rows(targets):
        return jnp.concatenate(
            [panel[pl.ds(al((sub * YS + t) * piece, piece), piece), :] for sub, t in targets], axis=0
        )

    def product(targets):
        prod[0 : len(targets) * piece, :] = jnp.dot(
            grad_rows(targets), cotp[...], preferred_element_type=F32
        )

    ring = {}

    def ring_start():
        opposite = (y + YS // 2) % YS
        product([(0, opposite), (1, opposite)])
        for h in range(2):
            for d in range(2):
                rs[d, h, 0, d] = prod[d * piece : (d + 1) * piece, h * half : (h + 1) * half].astype(BF16)
        for h in range(2):
            for d in range(2):
                ring[d, h, 0] = send(rs.at[d, h, 0, d], rr.at[d, h, 0, d], at_y(sides[d]))

    def ring_product(s):
        forward, backward = (y + YS // 2 - s) % YS, (y + YS // 2 + s) % YS
        product([(0, forward), (1, forward), (0, backward), (1, backward)])

    def ring_step(s):
        for h in range(2):
            for d in range(2):
                ring[d, h, s - 1].wait_recv()
                for sub in range(2):
                    at = (2 * d + sub) * piece
                    value = prod[at : at + piece, h * half : (h + 1) * half]
                    if s > 1 or sub == d:
                        value = value + rr[d, h, s - 1, sub].astype(F32)
                    rs[d, h, s, sub] = value.astype(BF16)
                ring[d, h, s] = send(rs.at[d, h, s], rr.at[d, h, s], at_y(sides[d]))

    last = YS // 2 - 1
    across = []

    def ring_end():
        for h in range(2):
            lanes = slice(h * half, (h + 1) * half)
            for d in range(2):
                ring[d, h, last].wait_recv()
            there = prod[piece : 2 * piece, lanes]
            there = there + rr[0, h, last, 1 - zh].astype(F32) + rr[1, h, last, 1 - zh].astype(F32)
            zs[h] = there.astype(BF16)
            across.append(send(zs.at[h], zr.at[h], partner))
            here = prod[0:piece, lanes]
            wg_ref[:, lanes] = here + rr[0, h, last, zh].astype(F32) + rr[1, h, last, zh].astype(F32)

    def out_pair(p):
        lhs = jnp.transpose(panel[:, pl.ds(al(p * pair, pair), pair)])
        ofull[...] = jnp.dot(lhs, w_ref[...], preferred_element_type=F32)
        osend[2 * p] = ofull[0:tokens, :].astype(BF16)
        osend[2 * p + 1] = ofull[tokens:pair, :].astype(BF16)

    ring_start()
    ring_product(1)
    second_hop = []
    for d in range(2):
        near = partial((x + sides[d] + XS) % XS)
        first_hop[d].wait_recv()
        for i in range(2):
            value = near[:, i * pair : (i + 1) * pair]
            if i == d:
                value = value + f1r[d].astype(F32)
            f2s[d, :, i * pair : (i + 1) * pair] = value.astype(BF16)
        second_hop.append(send(f2s.at[d], f2r.at[d], at_x(sides[d])))
    ring_step(1)
    out_pair(1 - col // 2)
    handed = send(osend.at[cols[2]], orecv.at[0], at_col(cols[1]))
    ring_product(2)
    back = partial(x)
    for d in range(2):
        second_hop[d].wait_recv()
        back = back + f2r[d].astype(F32)
    for c in range(blocks):
        gs[c] = back[:, c * tokens : (c + 1) * tokens].astype(BF16)
    turns = [send(gs.at[cols[k]], bl.at[col], at_col(cols[k])) for k in (1, 2, 3)]
    bl[col] = gs[col]
    ring_step(2)
    handed.wait_recv()
    osum[...] = (osend[cols[3]].astype(F32) + orecv[0].astype(F32)).astype(BF16)
    outs = [send(osum, orecv.at[1], at_col(cols[3]))]
    out_pair(col // 2)
    outs.append(send(osend.at[cols[1]], orecv.at[2], at_col(cols[1])))
    ring_product(3)
    ring_step(3)

    for copy in turns:
        copy.wait_recv()
    back = bl[...].astype(F32).reshape(blocks * share, tokens)
    scaled = back * gcol[...]
    hst[0:1, :] = jnp.sum(scaled, axis=0, keepdims=True)
    hst[1:2, :] = jnp.sum(scaled * normed[...], axis=0, keepdims=True)
    means = [send(hst, hstr.at[k], at_row((row + k) % n_row)) for k in range(1, n_row)]
    gcb[col] = jnp.sum(jnp.transpose(back * normed[...]), axis=0, keepdims=True)
    gain_cols = [send(gcb.at[col], gcb.at[col], at_col(cols[k])) for k in range(1, n_col)]
    product([(zh, y), (1 - zh, y)])
    for copy in gain_cols:
        copy.wait_recv()
    gzs[...] = gcb[0] + gcb[1] + gcb[2] + gcb[3]
    gain_z = send(gzs, gzr, partner)

    sums = hst[...]
    for k in range(1, n_row):
        means[k - 1].wait_recv()
        sums = sums + hstr[k]
    first = sums[0:1, :] / width
    second = sums[1:2, :] / width
    grad = inv_std * (bl[...].astype(F32).reshape(blocks * share, tokens) * gcol[...] - first - normed[...] * second)
    ig_ref[...] = grad.astype(BF16).reshape(blocks, share, tokens)
    ring_end()

    gain_z.wait_recv()
    gyb[y] = gzs[...] + gzr[...]
    gain_ys = [send(gyb.at[y], gyb.at[y], at_y(k)) for k in range(1, YS)]
    result = ofull[pl.ds(al((col % 2) * tokens, tokens), tokens), :]
    for i in range(2):
        outs[i].wait_recv()
        result = result + orecv[1 + i].astype(F32)
    out_ref[...] = result.astype(BF16)
    for copy in gain_ys:
        copy.wait_recv()
    group = gyb[0]
    for i in range(1, YS):
        group = group + gyb[i]
    group = group / n_dp
    for a in range(blocks):
        gg_ref[a : a + 1, :] = group[:, a * share : (a + 1) * share]
    for h in range(2):
        across[h].wait_recv()
        lanes = slice(h * half, (h + 1) * half)
        wg_ref[:, lanes] = (wg_ref[:, lanes] + zr[h].astype(F32)) / n_dp
    for copy in started:
        copy.wait_send()


def body(inputs, gain, weight, cotangent):
    tokens, blocks, share = inputs.shape[1:]
    part, wide = weight.shape
    n_dp, n_row, n_col = lax.axis_size("dp"), lax.axis_size("row"), lax.axis_size("col")
    piece = part // n_dp
    half = wide // 2
    pair = 2 * tokens
    vmem = pl.BlockSpec(memory_space=pltpu.VMEM)
    outputs, input_grad, gain_grad, weight_grad = pl.pallas_call(
        kernel,
        out_shape=(
            jax.ShapeDtypeStruct((tokens, wide), BF16),
            jax.ShapeDtypeStruct((blocks, share, tokens), BF16),
            jax.ShapeDtypeStruct((blocks, share), F32),
            jax.ShapeDtypeStruct((piece, wide), F32),
        ),
        in_specs=[vmem, vmem, pl.BlockSpec(memory_space=pl.ANY), vmem],
        out_specs=(vmem,) * 4,
        scratch_shapes=[
            pltpu.VMEM((2, tokens), F32),
            pltpu.VMEM((n_row, 2, tokens), F32),
            pltpu.VMEM((blocks * share, tokens), F32),
            pltpu.VMEM((blocks, share, tokens), BF16),
            pltpu.VMEM((blocks * share, tokens), F32),
            pltpu.VMEM((part, n_col * tokens), BF16),
            pltpu.VMEM((n_col * tokens, wide), BF16),
            pltpu.VMEM((part, n_col * tokens), BF16),
            pltpu.VMEM((XS, share, n_col * tokens), BF16),
            pltpu.VMEM((2, share, pair), BF16),
            pltpu.VMEM((2, share, pair), BF16),
            pltpu.VMEM((2, share, 2 * pair), BF16),
            pltpu.VMEM((2, share, 2 * pair), BF16),
            pltpu.VMEM((n_col, share, tokens), BF16),
            pltpu.VMEM((n_col, share, tokens), BF16),
            pltpu.VMEM((2, tokens), F32),
            pltpu.VMEM((n_row, 2, tokens), F32),
            pltpu.VMEM((n_col, tokens, wide), BF16),
            pltpu.VMEM((3, tokens, wide), BF16),
            pltpu.VMEM((tokens, wide), BF16),
            pltpu.VMEM((pair, wide), F32),
            pltpu.VMEM((part, wide), BF16),
            pltpu.VMEM((4 * piece, wide), F32),
            pltpu.VMEM((2, 2, YS // 2, 2, piece, half), BF16),
            pltpu.VMEM((2, 2, YS // 2, 2, piece, half), BF16),
            pltpu.VMEM((2, piece, half), BF16),
            pltpu.VMEM((2, piece, half), BF16),
            pltpu.VMEM((n_col, 1, blocks * share), F32),
            pltpu.VMEM((YS, 1, blocks * share), F32),
            pltpu.VMEM((1, blocks * share), F32),
            pltpu.VMEM((1, blocks * share), F32),
            pltpu.SemaphoreType.DMA((COPIES,)),
            pltpu.SemaphoreType.DMA((COPIES,)),
            pltpu.SemaphoreType.DMA,
        ],
        compiler_params=pltpu.CompilerParams(collective_id=0, has_side_effects=True),
    )(
        jnp.transpose(inputs[0], (1, 2, 0)),
        gain,
        weight,
        cotangent[0],
    )
    return (
        outputs[None],
        jnp.transpose(input_grad, (2, 0, 1))[None],
        gain_grad,
        weight_grad[None],
    )


def solution(mesh):
    return jax.shard_map(
        body,
        mesh=mesh,
        in_specs=(
            P("dp", "col", None, "row"),
            P(None, "row"),
            P("col", "row"),
            P("dp", "col", "row"),
        ),
        out_specs=(
            P("dp", "col", "row"),
            P("dp", "col", None, "row"),
            P(None, "row"),
            P("col", "dp", "row"),
        ),
        check_vma=False,
    )
```

```python
import functools

import jax
import jax.numpy as jnp
from jax import lax
from jax.experimental import pallas as pl
from jax.experimental.pallas import tpu as pltpu
from jax.sharding import PartitionSpec as P

EPS = 1e-05
F32 = jnp.float32
BF16 = jnp.bfloat16
YS = 8
XS = 4
COPIES = 96


def al(value, to):
    return pl.multiple_of(value, to)


def kernel(
    x_ref, g_ref, w_hbm, cot_ref,
    out_ref, ig_ref, gg_ref, wg_ref,
    stat, statr, normed, hid, gcol, panel, cotp, bsend, sibr,
    f1s, f1r, f2s, f2r, gs, bl, hst, hstr, osend, orecv, osum, ofull, w_ref,
    prod, rs, rr, zs, zr, gcb, gyb, gzs, gzr, ssem, rsem, wsem,
):
    blocks, share, tokens = x_ref.shape
    wide = cot_ref.shape[1]
    n_row, n_col, n_dp = lax.axis_size("row"), lax.axis_size("col"), lax.axis_size("dp")
    part = n_row * share
    width = n_row * blocks * share
    piece = part // n_dp
    half = wide // 2
    pair = 2 * tokens

    dp, row, col = lax.axis_index("dp"), lax.axis_index("row"), lax.axis_index("col")
    zh, y = dp // YS, dp % YS
    x, core = row // 2, row % 2
    cols = [col, col + 1 - 2 * (col % 2), (col + 2) % n_col, n_col - 1 - col]

    def at_row(r):
        return {"row": r}

    def at_x(step):
        return {"row": ((x + step + XS) % XS) * 2 + core}

    def at_col(c):
        return {"col": c}

    def at_y(step):
        return {"dp": zh * YS + (y + step + YS) % YS}

    sibling = {"row": x * 2 + 1 - core}
    partner = {"dp": (dp + YS) % n_dp}

    weight_in = pltpu.make_async_copy(w_hbm, w_ref, wsem)
    weight_in.start()
    started = []

    def send(src, dst, device):
        index = len(started)
        copy = pltpu.make_async_remote_copy(
            src_ref=src,
            dst_ref=dst,
            send_sem=ssem.at[index],
            recv_sem=rsem.at[index],
            device_id=device,
            device_id_type=pl.DeviceIdType.MESH,
        )
        copy.start()
        started.append(copy)
        return copy

    barrier = pltpu.get_barrier_semaphore()
    peers = [at_row((row + k) % n_row) for k in range(1, n_row)]
    peers += [at_col(cols[k]) for k in range(1, n_col)]
    peers += [at_y(k) for k in range(1, YS)]
    peers += [partner]
    for peer in peers:
        pl.semaphore_signal(barrier, inc=1, device_id=peer, device_id_type=pl.DeviceIdType.MESH)

    values = x_ref[...].astype(F32)
    stat[0:1, :] = jnp.sum(values, axis=(0, 1)).reshape(1, tokens)
    stat[1:2, :] = jnp.sum(values * values, axis=(0, 1)).reshape(1, tokens)
    cotp[pl.ds(al(col * tokens, tokens), tokens), :] = cot_ref[...]
    pl.semaphore_wait(barrier, len(peers))

    own_rows = pl.ds(al(col * tokens, tokens), tokens)
    stats = [send(stat, statr.at[k], at_row((row + k) % n_row)) for k in range(1, n_row)]
    beside = send(cot_ref, cotp.at[own_rows, :], at_col(cols[1]))
    gain = g_ref[...].astype(F32)
    for a in range(blocks):
        gcol[a * share : (a + 1) * share, :] = jnp.transpose(
            jnp.broadcast_to(gain[a : a + 1, :], (tokens, share))
        )

    total = stat[...]
    for k in range(1, n_row):
        stats[k - 1].wait_recv()
        total = total + statr[k]
    mean = total[0:1, :] / width
    variance = total[1:2, :] / width - mean * mean
    inv_std = lax.rsqrt(variance + EPS)
    flat = x_ref[...].astype(F32).reshape(blocks * share, tokens)
    norm = (flat - mean) * inv_std
    normed[...] = norm
    hid[...] = (norm * gcol[...]).astype(BF16).reshape(blocks, share, tokens)

    mine = pl.ds(al(row * share, share), share)
    own_lanes = pl.ds(al(col * tokens, tokens), tokens)
    moves = {k: send(hid.at[cols[k]], panel.at[mine, own_lanes], at_col(cols[k])) for k in (1, 3, 2)}
    panel[mine, own_lanes] = hid[col]
    few = tokens // 2
    across_col = []
    for i in range(2):
        at = pl.ds(al(col * tokens + i * few, few), few)
        across_col.append(send(cot_ref.at[pl.ds(i * few, few), :], cotp.at[at, :], at_col(cols[3])))

    def back_pair(p):
        lanes = pl.ds(al(p * pair, pair), pair)
        rhs_rows = pl.ds(al(p * pair, pair), pair)
        step = part // 2

        @pl.loop(0, 2)
        def _(i):
            rows = pl.ds(al(i * step, step), step)
            bsend[rows, lanes] = lax.dot_general(
                w_ref[rows, :], cotp[rhs_rows, :], (((1,), (1,)), ((), ())), preferred_element_type=F32
            ).astype(BF16)

        return [
            send(
                bsend.at[pl.ds(al((2 * xd + 1 - core) * share, share), share), lanes],
                sibr.at[xd, :, lanes],
                sibling,
            )
            for xd in range(XS)
        ]

    beside.wait_recv()
    weight_in.wait()
    sibs = back_pair(col // 2)

    for k in (1, 3, 2):
        moves[k].wait_recv()

    def block_of(step):
        return pl.ds(al((((x + step + XS) % XS) * 2 + core) * share, share), share)

    low, high = pl.ds(0, pair), pl.ds(pair, pair)
    right = [send(panel.at[mine, part_of], panel.at[mine, part_of], at_x(1)) for part_of in (low, high)]
    left = [send(panel.at[mine, part_of], panel.at[mine, part_of], at_x(-1)) for part_of in (high, low)]
    gathers = [send(panel.at[mine, :], panel.at[mine, :], sibling)]
    passed = []
    for i in range(2):
        across_col[i].wait_recv()
        at = pl.ds(al(cols[3] * tokens + i * few, few), few)
        passed.append(send(cotp.at[at, :], cotp.at[at, :], at_col(cols[1])))
        if i == 0:
            right[0].wait_recv()
            relay_right = send(panel.at[block_of(-1), low], panel.at[block_of(-1), low], at_x(1))
            left[0].wait_recv()
            relay_left = send(panel.at[block_of(1), high], panel.at[block_of(1), high], at_x(-1))
    right[1].wait_recv()
    gathers.append(send(panel.at[block_of(-1), :], panel.at[block_of(-1), :], sibling))
    left[1].wait_recv()
    gathers.append(send(panel.at[block_of(1), :], panel.at[block_of(1), :], sibling))
    relay_right.wait_recv()
    gathers.append(send(panel.at[block_of(2), low], panel.at[block_of(2), low], sibling))
    relay_left.wait_recv()
    gathers.append(send(panel.at[block_of(2), high], panel.at[block_of(2), high], sibling))

    def partial(xd):
        rows = pl.ds(al((2 * xd + core) * share, share), share)
        return bsend[rows, :].astype(F32) + sibr[xd].astype(F32)

    sides = (1, -1)
    for copy in passed:
        copy.wait_recv()
    sibs += back_pair(1 - col // 2)
    for copy in sibs:
        copy.wait_recv()
    far = partial((x + 2) % XS)
    f1s[0] = far[:, 0:pair].astype(BF16)
    f1s[1] = far[:, pair : 2 * pair].astype(BF16)
    first_hop = [send(f1s.at[d], f1r.at[d], at_x(sides[d])) for d in range(2)]
    for copy in gathers:
        copy.wait_recv()

    def grad_rows(targets):
        return jnp.concatenate(
            [panel[pl.ds(al((sub * YS + t) * piece, piece), piece), :] for sub, t in targets], axis=0
        )

    def product(targets):
        prod[0 : len(targets) * piece, :] = jnp.dot(
            grad_rows(targets), cotp[...], preferred_element_type=F32
        )

    ring = {}

    def ring_start():
        opposite = (y + YS // 2) % YS
        product([(0, opposite), (1, opposite)])
        for h in range(2):
            for d in range(2):
                rs[d, h, 0, d] = prod[d * piece : (d + 1) * piece, h * half : (h + 1) * half].astype(BF16)
        for h in range(2):
            for d in range(2):
                ring[d, h, 0] = send(rs.at[d, h, 0, d], rr.at[d, h, 0, d], at_y(sides[d]))

    def ring_product(s):
        forward, backward = (y + YS // 2 - s) % YS, (y + YS // 2 + s) % YS
        product([(0, forward), (1, forward), (0, backward), (1, backward)])

    def ring_step(s):
        for h in range(2):
            for d in range(2):
                ring[d, h, s - 1].wait_recv()
                for sub in range(2):
                    at = (2 * d + sub) * piece
                    value = prod[at : at + piece, h * half : (h + 1) * half]
                    if s > 1 or sub == d:
                        value = value + rr[d, h, s - 1, sub].astype(F32)
                    rs[d, h, s, sub] = value.astype(BF16)
                ring[d, h, s] = send(rs.at[d, h, s], rr.at[d, h, s], at_y(sides[d]))

    last = YS // 2 - 1
    across = []

    def ring_end():
        for h in range(2):
            lanes = slice(h * half, (h + 1) * half)
            for d in range(2):
                ring[d, h, last].wait_recv()
            there = prod[piece : 2 * piece, lanes]
            there = there + rr[0, h, last, 1 - zh].astype(F32) + rr[1, h, last, 1 - zh].astype(F32)
            zs[h] = there.astype(BF16)
            across.append(send(zs.at[h], zr.at[h], partner))
            here = prod[0:piece, lanes]
            wg_ref[:, lanes] = here + rr[0, h, last, zh].astype(F32) + rr[1, h, last, zh].astype(F32)

    def out_pair(p):
        lhs = jnp.transpose(panel[:, pl.ds(al(p * pair, pair), pair)])
        ofull[...] = jnp.dot(lhs, w_ref[...], preferred_element_type=F32)
        osend[2 * p] = ofull[0:tokens, :].astype(BF16)
        osend[2 * p + 1] = ofull[tokens:pair, :].astype(BF16)

    ring_start()
    ring_product(1)
    second_hop = []
    for d in range(2):
        near = partial((x + sides[d] + XS) % XS)
        first_hop[d].wait_recv()
        for i in range(2):
            value = near[:, i * pair : (i + 1) * pair]
            if i == d:
                value = value + f1r[d].astype(F32)
            f2s[d, :, i * pair : (i + 1) * pair] = value.astype(BF16)
        second_hop.append(send(f2s.at[d], f2r.at[d], at_x(sides[d])))
    ring_step(1)
    out_pair(1 - col // 2)
    handed = send(osend.at[cols[2]], orecv.at[0], at_col(cols[1]))
    ring_product(2)
    back = partial(x)
    for d in range(2):
        second_hop[d].wait_recv()
        back = back + f2r[d].astype(F32)
    for c in range(blocks):
        gs[c] = back[:, c * tokens : (c + 1) * tokens].astype(BF16)
    turns = [send(gs.at[cols[k]], bl.at[col], at_col(cols[k])) for k in (1, 2, 3)]
    bl[col] = gs[col]
    ring_step(2)
    handed.wait_recv()
    osum[...] = (osend[cols[3]].astype(F32) + orecv[0].astype(F32)).astype(BF16)
    outs = [send(osum, orecv.at[1], at_col(cols[3]))]
    out_pair(col // 2)
    outs.append(send(osend.at[cols[1]], orecv.at[2], at_col(cols[1])))
    ring_product(3)
    ring_step(3)

    for copy in turns:
        copy.wait_recv()
    back = bl[...].astype(F32).reshape(blocks * share, tokens)
    scaled = back * gcol[...]
    hst[0:1, :] = jnp.sum(scaled, axis=0, keepdims=True)
    hst[1:2, :] = jnp.sum(scaled * normed[...], axis=0, keepdims=True)
    means = [send(hst, hstr.at[k], at_row((row + k) % n_row)) for k in range(1, n_row)]
    gcb[col] = jnp.sum(jnp.transpose(back * normed[...]), axis=0, keepdims=True)
    gain_cols = [send(gcb.at[col], gcb.at[col], at_col(cols[k])) for k in range(1, n_col)]
    product([(zh, y), (1 - zh, y)])
    for copy in gain_cols:
        copy.wait_recv()
    gzs[...] = gcb[0] + gcb[1] + gcb[2] + gcb[3]
    gain_z = send(gzs, gzr, partner)

    sums = hst[...]
    for k in range(1, n_row):
        means[k - 1].wait_recv()
        sums = sums + hstr[k]
    first = sums[0:1, :] / width
    second = sums[1:2, :] / width
    grad = inv_std * (bl[...].astype(F32).reshape(blocks * share, tokens) * gcol[...] - first - normed[...] * second)
    ig_ref[...] = grad.astype(BF16).reshape(blocks, share, tokens)
    ring_end()

    gain_z.wait_recv()
    gyb[y] = gzs[...] + gzr[...]
    gain_ys = [send(gyb.at[y], gyb.at[y], at_y(k)) for k in range(1, YS)]
    result = ofull[pl.ds(al((col % 2) * tokens, tokens), tokens), :]
    for i in range(2):
        outs[i].wait_recv()
        result = result + orecv[1 + i].astype(F32)
    out_ref[...] = result.astype(BF16)
    for copy in gain_ys:
        copy.wait_recv()
    group = gyb[0]
    for i in range(1, YS):
        group = group + gyb[i]
    group = group / n_dp
    for a in range(blocks):
        gg_ref[a : a + 1, :] = group[:, a * share : (a + 1) * share]
    for h in range(2):
        across[h].wait_recv()
        lanes = slice(h * half, (h + 1) * half)
        wg_ref[:, lanes] = (wg_ref[:, lanes] + zr[h].astype(F32)) / n_dp
    for copy in started:
        copy.wait_send()


def hand_out(*refs):
    n = (len(refs) - 2) // 3
    sources, targets, held = refs[:n], refs[n : 2 * n], refs[2 * n : 3 * n]
    isem, osem = refs[3 * n :]
    reads = [pltpu.make_async_copy(sources[i], held[i], isem.at[i]) for i in range(n)]
    writes = [pltpu.make_async_copy(held[i], targets[i], osem.at[i]) for i in range(n)]
    for copy in reads:
        copy.start()
    for i in range(n):
        reads[i].wait()
        writes[i].start()
    for copy in writes:
        copy.wait()


def body(inputs, gain, weight, cotangent):
    tokens, blocks, share = inputs.shape[1:]
    part, wide = weight.shape
    n_dp, n_row, n_col = lax.axis_size("dp"), lax.axis_size("row"), lax.axis_size("col")
    piece = part // n_dp
    half = wide // 2
    pair = 2 * tokens
    vmem = pl.BlockSpec(memory_space=pltpu.VMEM)
    results = pl.pallas_call(
        kernel,
        out_shape=(
            jax.ShapeDtypeStruct((tokens, wide), BF16),
            jax.ShapeDtypeStruct((blocks, share, tokens), BF16),
            jax.ShapeDtypeStruct((blocks, share), F32),
            jax.ShapeDtypeStruct((piece, wide), F32),
        ),
        in_specs=[vmem, vmem, pl.BlockSpec(memory_space=pl.ANY), vmem],
        out_specs=(vmem,) * 4,
        scratch_shapes=[
            pltpu.VMEM((2, tokens), F32),
            pltpu.VMEM((n_row, 2, tokens), F32),
            pltpu.VMEM((blocks * share, tokens), F32),
            pltpu.VMEM((blocks, share, tokens), BF16),
            pltpu.VMEM((blocks * share, tokens), F32),
            pltpu.VMEM((part, n_col * tokens), BF16),
            pltpu.VMEM((n_col * tokens, wide), BF16),
            pltpu.VMEM((part, n_col * tokens), BF16),
            pltpu.VMEM((XS, share, n_col * tokens), BF16),
            pltpu.VMEM((2, share, pair), BF16),
            pltpu.VMEM((2, share, pair), BF16),
            pltpu.VMEM((2, share, 2 * pair), BF16),
            pltpu.VMEM((2, share, 2 * pair), BF16),
            pltpu.VMEM((n_col, share, tokens), BF16),
            pltpu.VMEM((n_col, share, tokens), BF16),
            pltpu.VMEM((2, tokens), F32),
            pltpu.VMEM((n_row, 2, tokens), F32),
            pltpu.VMEM((n_col, tokens, wide), BF16),
            pltpu.VMEM((3, tokens, wide), BF16),
            pltpu.VMEM((tokens, wide), BF16),
            pltpu.VMEM((pair, wide), F32),
            pltpu.VMEM((part, wide), BF16),
            pltpu.VMEM((4 * piece, wide), F32),
            pltpu.VMEM((2, 2, YS // 2, 2, piece, half), BF16),
            pltpu.VMEM((2, 2, YS // 2, 2, piece, half), BF16),
            pltpu.VMEM((2, piece, half), BF16),
            pltpu.VMEM((2, piece, half), BF16),
            pltpu.VMEM((n_col, 1, blocks * share), F32),
            pltpu.VMEM((YS, 1, blocks * share), F32),
            pltpu.VMEM((1, blocks * share), F32),
            pltpu.VMEM((1, blocks * share), F32),
            pltpu.SemaphoreType.DMA((COPIES,)),
            pltpu.SemaphoreType.DMA((COPIES,)),
            pltpu.SemaphoreType.DMA,
        ],
        compiler_params=pltpu.CompilerParams(collective_id=0, has_side_effects=True),
    )(
        jnp.transpose(inputs[0], (1, 2, 0)),
        gain,
        weight,
        cotangent[0],
    )
    anywhere = pl.BlockSpec(memory_space=pl.ANY)
    outputs, input_grad, gain_grad, weight_grad = pl.pallas_call(
        hand_out,
        out_shape=tuple(jax.ShapeDtypeStruct(r.shape, r.dtype) for r in results),
        in_specs=[anywhere] * len(results),
        out_specs=(anywhere,) * len(results),
        scratch_shapes=[pltpu.VMEM(r.shape, r.dtype) for r in results]
        + [pltpu.SemaphoreType.DMA((len(results),)), pltpu.SemaphoreType.DMA((len(results),))],
    )(*results)
    return (
        outputs[None],
        jnp.transpose(input_grad, (2, 0, 1))[None],
        gain_grad,
        weight_grad[None],
    )


def solution(mesh):
    return jax.shard_map(
        body,
        mesh=mesh,
        in_specs=(
            P("dp", "col", None, "row"),
            P(None, "row"),
            P("col", "row"),
            P("dp", "col", "row"),
        ),
        out_specs=(
            P("dp", "col", "row"),
            P("dp", "col", None, "row"),
            P(None, "row"),
            P("col", "dp", "row"),
        ),
        check_vma=False,
    )
```

```python
import functools

import jax
import jax.numpy as jnp
from jax import lax
from jax.experimental import pallas as pl
from jax.experimental.pallas import tpu as pltpu
from jax.sharding import PartitionSpec as P

EPS = 1e-05
F32 = jnp.float32
BF16 = jnp.bfloat16
YS = 8
XS = 4
COPIES = 96


def al(value, to):
    return pl.multiple_of(value, to)


def kernel(
    x_ref, g_ref, w_hbm, cot_ref,
    out_ref, ig_ref, gg_ref, wg_ref,
    stat, statr, normed, hid, gcol, panel, cotp, bsend, sibr,
    f1s, f1r, f2s, f2r, gs, bl, hst, hstr, osend, orecv, osum, ofull, w_ref,
    prod, rs, rr, zs, zr, gcb, gyb, gzs, gzr, ssem, rsem, wsem,
):
    blocks, share, tokens = x_ref.shape
    wide = cot_ref.shape[1]
    n_row, n_col, n_dp = lax.axis_size("row"), lax.axis_size("col"), lax.axis_size("dp")
    part = n_row * share
    width = n_row * blocks * share
    piece = part // n_dp
    half = wide // 2
    pair = 2 * tokens

    dp, row, col = lax.axis_index("dp"), lax.axis_index("row"), lax.axis_index("col")
    zh, y = dp // YS, dp % YS
    x, core = row // 2, row % 2
    cols = [col, col + 1 - 2 * (col % 2), (col + 2) % n_col, n_col - 1 - col]

    def at_row(r):
        return {"row": r}

    def at_x(step):
        return {"row": ((x + step + XS) % XS) * 2 + core}

    def at_col(c):
        return {"col": c}

    def at_y(step):
        return {"dp": zh * YS + (y + step + YS) % YS}

    sibling = {"row": x * 2 + 1 - core}
    partner = {"dp": (dp + YS) % n_dp}

    weight_in = pltpu.make_async_copy(w_hbm, w_ref, wsem)
    weight_in.start()
    started = []

    def send(src, dst, device):
        index = len(started)
        copy = pltpu.make_async_remote_copy(
            src_ref=src,
            dst_ref=dst,
            send_sem=ssem.at[index],
            recv_sem=rsem.at[index],
            device_id=device,
            device_id_type=pl.DeviceIdType.MESH,
        )
        copy.start()
        started.append(copy)
        return copy

    barrier = pltpu.get_barrier_semaphore()
    peers = [at_row((row + k) % n_row) for k in range(1, n_row)]
    peers += [at_col(cols[k]) for k in range(1, n_col)]
    peers += [at_y(k) for k in range(1, YS)]
    peers += [partner]
    for peer in peers:
        pl.semaphore_signal(barrier, inc=1, device_id=peer, device_id_type=pl.DeviceIdType.MESH)

    values = x_ref[...].astype(F32)
    stat[0:1, :] = jnp.sum(values, axis=(0, 1)).reshape(1, tokens)
    stat[1:2, :] = jnp.sum(values * values, axis=(0, 1)).reshape(1, tokens)
    cotp[pl.ds(al(col * tokens, tokens), tokens), :] = cot_ref[...]
    pl.semaphore_wait(barrier, len(peers))

    own_rows = pl.ds(al(col * tokens, tokens), tokens)
    stats = [send(stat, statr.at[k], at_row((row + k) % n_row)) for k in range(1, n_row)]
    beside = send(cot_ref, cotp.at[own_rows, :], at_col(cols[1]))
    gain = g_ref[...].astype(F32)
    for a in range(blocks):
        gcol[a * share : (a + 1) * share, :] = jnp.transpose(
            jnp.broadcast_to(gain[a : a + 1, :], (tokens, share))
        )

    total = stat[...]
    for k in range(1, n_row):
        stats[k - 1].wait_recv()
        total = total + statr[k]
    mean = total[0:1, :] / width
    variance = total[1:2, :] / width - mean * mean
    inv_std = lax.rsqrt(variance + EPS)
    flat = x_ref[...].astype(F32).reshape(blocks * share, tokens)
    norm = (flat - mean) * inv_std
    normed[...] = norm
    hid[...] = (norm * gcol[...]).astype(BF16).reshape(blocks, share, tokens)

    mine = pl.ds(al(row * share, share), share)
    own_lanes = pl.ds(al(col * tokens, tokens), tokens)
    moves = {k: send(hid.at[cols[k]], panel.at[mine, own_lanes], at_col(cols[k])) for k in (1, 3, 2)}
    panel[mine, own_lanes] = hid[col]
    few = tokens // 2
    across_col = []
    for i in range(2):
        at = pl.ds(al(col * tokens + i * few, few), few)
        across_col.append(send(cot_ref.at[pl.ds(i * few, few), :], cotp.at[at, :], at_col(cols[3])))

    def back_pair(p):
        lanes = pl.ds(al(p * pair, pair), pair)
        rhs_rows = pl.ds(al(p * pair, pair), pair)
        step = part // 2

        @pl.loop(0, 2)
        def _(i):
            rows = pl.ds(al(i * step, step), step)
            bsend[rows, lanes] = lax.dot_general(
                w_ref[rows, :], cotp[rhs_rows, :], (((1,), (1,)), ((), ())), preferred_element_type=F32
            ).astype(BF16)

        return [
            send(
                bsend.at[pl.ds(al((2 * xd + 1 - core) * share, share), share), lanes],
                sibr.at[xd, :, lanes],
                sibling,
            )
            for xd in range(XS)
        ]

    beside.wait_recv()
    weight_in.wait()
    sibs = back_pair(col // 2)

    for k in (1, 3, 2):
        moves[k].wait_recv()

    def block_of(step):
        return pl.ds(al((((x + step + XS) % XS) * 2 + core) * share, share), share)

    low, high = pl.ds(0, pair), pl.ds(pair, pair)
    right = [send(panel.at[mine, part_of], panel.at[mine, part_of], at_x(1)) for part_of in (low, high)]
    left = [send(panel.at[mine, part_of], panel.at[mine, part_of], at_x(-1)) for part_of in (high, low)]
    gathers = [send(panel.at[mine, :], panel.at[mine, :], sibling)]
    passed = []
    for i in range(2):
        across_col[i].wait_recv()
        at = pl.ds(al(cols[3] * tokens + i * few, few), few)
        passed.append(send(cotp.at[at, :], cotp.at[at, :], at_col(cols[1])))
        if i == 0:
            right[0].wait_recv()
            relay_right = send(panel.at[block_of(-1), low], panel.at[block_of(-1), low], at_x(1))
            left[0].wait_recv()
            relay_left = send(panel.at[block_of(1), high], panel.at[block_of(1), high], at_x(-1))
    right[1].wait_recv()
    gathers.append(send(panel.at[block_of(-1), :], panel.at[block_of(-1), :], sibling))
    left[1].wait_recv()
    gathers.append(send(panel.at[block_of(1), :], panel.at[block_of(1), :], sibling))
    relay_right.wait_recv()
    gathers.append(send(panel.at[block_of(2), low], panel.at[block_of(2), low], sibling))
    relay_left.wait_recv()
    gathers.append(send(panel.at[block_of(2), high], panel.at[block_of(2), high], sibling))

    def partial(xd):
        rows = pl.ds(al((2 * xd + core) * share, share), share)
        return bsend[rows, :].astype(F32) + sibr[xd].astype(F32)

    sides = (1, -1)
    for copy in passed:
        copy.wait_recv()
    for copy in gathers:
        copy.wait_recv()

    def grad_rows(targets):
        return jnp.concatenate(
            [panel[pl.ds(al((sub * YS + t) * piece, piece), piece), :] for sub, t in targets], axis=0
        )

    def product(targets):
        prod[0 : len(targets) * piece, :] = jnp.dot(
            grad_rows(targets), cotp[...], preferred_element_type=F32
        )

    ring = {}

    def ring_start():
        opposite = (y + YS // 2) % YS
        product([(0, opposite), (1, opposite)])
        for h in range(2):
            for d in range(2):
                rs[d, h, 0, d] = prod[d * piece : (d + 1) * piece, h * half : (h + 1) * half].astype(BF16)
        for h in range(2):
            for d in range(2):
                ring[d, h, 0] = send(rs.at[d, h, 0, d], rr.at[d, h, 0, d], at_y(sides[d]))

    def ring_product(s):
        forward, backward = (y + YS // 2 - s) % YS, (y + YS // 2 + s) % YS
        product([(0, forward), (1, forward), (0, backward), (1, backward)])

    def ring_step(s):
        for h in range(2):
            for d in range(2):
                ring[d, h, s - 1].wait_recv()
                for sub in range(2):
                    at = (2 * d + sub) * piece
                    value = prod[at : at + piece, h * half : (h + 1) * half]
                    if s > 1 or sub == d:
                        value = value + rr[d, h, s - 1, sub].astype(F32)
                    rs[d, h, s, sub] = value.astype(BF16)
                ring[d, h, s] = send(rs.at[d, h, s], rr.at[d, h, s], at_y(sides[d]))

    last = YS // 2 - 1
    across = []

    def ring_end():
        for h in range(2):
            lanes = slice(h * half, (h + 1) * half)
            for d in range(2):
                ring[d, h, last].wait_recv()
            there = prod[piece : 2 * piece, lanes]
            there = there + rr[0, h, last, 1 - zh].astype(F32) + rr[1, h, last, 1 - zh].astype(F32)
            zs[h] = there.astype(BF16)
            across.append(send(zs.at[h], zr.at[h], partner))
            here = prod[0:piece, lanes]
            wg_ref[:, lanes] = here + rr[0, h, last, zh].astype(F32) + rr[1, h, last, zh].astype(F32)

    def out_pair(p):
        lhs = jnp.transpose(panel[:, pl.ds(al(p * pair, pair), pair)])
        ofull[...] = jnp.dot(lhs, w_ref[...], preferred_element_type=F32)
        osend[2 * p] = ofull[0:tokens, :].astype(BF16)
        osend[2 * p + 1] = ofull[tokens:pair, :].astype(BF16)

    ring_start()
    sibs += back_pair(1 - col // 2)
    ring_product(1)
    ring_step(1)
    for copy in sibs:
        copy.wait_recv()
    far = partial((x + 2) % XS)
    f1s[0] = far[:, 0:pair].astype(BF16)
    f1s[1] = far[:, pair : 2 * pair].astype(BF16)
    first_hop = [send(f1s.at[d], f1r.at[d], at_x(sides[d])) for d in range(2)]
    out_pair(1 - col // 2)
    handed = send(osend.at[cols[2]], orecv.at[0], at_col(cols[1]))
    second_hop = []
    for d in range(2):
        near = partial((x + sides[d] + XS) % XS)
        first_hop[d].wait_recv()
        for i in range(2):
            value = near[:, i * pair : (i + 1) * pair]
            if i == d:
                value = value + f1r[d].astype(F32)
            f2s[d, :, i * pair : (i + 1) * pair] = value.astype(BF16)
        second_hop.append(send(f2s.at[d], f2r.at[d], at_x(sides[d])))
    ring_product(2)
    ring_step(2)
    back = partial(x)
    for d in range(2):
        second_hop[d].wait_recv()
        back = back + f2r[d].astype(F32)
    for c in range(blocks):
        gs[c] = back[:, c * tokens : (c + 1) * tokens].astype(BF16)
    turns = [send(gs.at[cols[k]], bl.at[col], at_col(cols[k])) for k in (1, 2, 3)]
    bl[col] = gs[col]
    handed.wait_recv()
    osum[...] = (osend[cols[3]].astype(F32) + orecv[0].astype(F32)).astype(BF16)
    outs = [send(osum, orecv.at[1], at_col(cols[3]))]
    out_pair(col // 2)
    outs.append(send(osend.at[cols[1]], orecv.at[2], at_col(cols[1])))
    ring_product(3)
    ring_step(3)

    for copy in turns:
        copy.wait_recv()
    back = bl[...].astype(F32).reshape(blocks * share, tokens)
    scaled = back * gcol[...]
    hst[0:1, :] = jnp.sum(scaled, axis=0, keepdims=True)
    hst[1:2, :] = jnp.sum(scaled * normed[...], axis=0, keepdims=True)
    means = [send(hst, hstr.at[k], at_row((row + k) % n_row)) for k in range(1, n_row)]
    gcb[col] = jnp.sum(jnp.transpose(back * normed[...]), axis=0, keepdims=True)
    gain_cols = [send(gcb.at[col], gcb.at[col], at_col(cols[k])) for k in range(1, n_col)]
    product([(zh, y), (1 - zh, y)])
    for copy in gain_cols:
        copy.wait_recv()
    gzs[...] = gcb[0] + gcb[1] + gcb[2] + gcb[3]
    gain_z = send(gzs, gzr, partner)

    sums = hst[...]
    for k in range(1, n_row):
        means[k - 1].wait_recv()
        sums = sums + hstr[k]
    first = sums[0:1, :] / width
    second = sums[1:2, :] / width
    grad = inv_std * (bl[...].astype(F32).reshape(blocks * share, tokens) * gcol[...] - first - normed[...] * second)
    ig_ref[...] = grad.astype(BF16).reshape(blocks, share, tokens)
    ring_end()

    gain_z.wait_recv()
    gyb[y] = gzs[...] + gzr[...]
    gain_ys = [send(gyb.at[y], gyb.at[y], at_y(k)) for k in range(1, YS)]
    result = ofull[pl.ds(al((col % 2) * tokens, tokens), tokens), :]
    for i in range(2):
        outs[i].wait_recv()
        result = result + orecv[1 + i].astype(F32)
    out_ref[...] = result.astype(BF16)
    for copy in gain_ys:
        copy.wait_recv()
    group = gyb[0]
    for i in range(1, YS):
        group = group + gyb[i]
    group = group / n_dp
    for a in range(blocks):
        gg_ref[a : a + 1, :] = group[:, a * share : (a + 1) * share]
    for h in range(2):
        across[h].wait_recv()
        lanes = slice(h * half, (h + 1) * half)
        wg_ref[:, lanes] = (wg_ref[:, lanes] + zr[h].astype(F32)) / n_dp
    for copy in started:
        copy.wait_send()


def hand_out(*refs):
    n = (len(refs) - 2) // 3
    sources, targets, held = refs[:n], refs[n : 2 * n], refs[2 * n : 3 * n]
    isem, osem = refs[3 * n :]
    reads = [pltpu.make_async_copy(sources[i], held[i], isem.at[i]) for i in range(n)]
    writes = [pltpu.make_async_copy(held[i], targets[i], osem.at[i]) for i in range(n)]
    for copy in reads:
        copy.start()
    for i in range(n):
        reads[i].wait()
        writes[i].start()
    for copy in writes:
        copy.wait()


def body(inputs, gain, weight, cotangent):
    tokens, blocks, share = inputs.shape[1:]
    part, wide = weight.shape
    n_dp, n_row, n_col = lax.axis_size("dp"), lax.axis_size("row"), lax.axis_size("col")
    piece = part // n_dp
    half = wide // 2
    pair = 2 * tokens
    vmem = pl.BlockSpec(memory_space=pltpu.VMEM)
    results = pl.pallas_call(
        kernel,
        out_shape=(
            jax.ShapeDtypeStruct((tokens, wide), BF16),
            jax.ShapeDtypeStruct((blocks, share, tokens), BF16),
            jax.ShapeDtypeStruct((blocks, share), F32),
            jax.ShapeDtypeStruct((piece, wide), F32),
        ),
        in_specs=[vmem, vmem, pl.BlockSpec(memory_space=pl.ANY), vmem],
        out_specs=(vmem,) * 4,
        scratch_shapes=[
            pltpu.VMEM((2, tokens), F32),
            pltpu.VMEM((n_row, 2, tokens), F32),
            pltpu.VMEM((blocks * share, tokens), F32),
            pltpu.VMEM((blocks, share, tokens), BF16),
            pltpu.VMEM((blocks * share, tokens), F32),
            pltpu.VMEM((part, n_col * tokens), BF16),
            pltpu.VMEM((n_col * tokens, wide), BF16),
            pltpu.VMEM((part, n_col * tokens), BF16),
            pltpu.VMEM((XS, share, n_col * tokens), BF16),
            pltpu.VMEM((2, share, pair), BF16),
            pltpu.VMEM((2, share, pair), BF16),
            pltpu.VMEM((2, share, 2 * pair), BF16),
            pltpu.VMEM((2, share, 2 * pair), BF16),
            pltpu.VMEM((n_col, share, tokens), BF16),
            pltpu.VMEM((n_col, share, tokens), BF16),
            pltpu.VMEM((2, tokens), F32),
            pltpu.VMEM((n_row, 2, tokens), F32),
            pltpu.VMEM((n_col, tokens, wide), BF16),
            pltpu.VMEM((3, tokens, wide), BF16),
            pltpu.VMEM((tokens, wide), BF16),
            pltpu.VMEM((pair, wide), F32),
            pltpu.VMEM((part, wide), BF16),
            pltpu.VMEM((4 * piece, wide), F32),
            pltpu.VMEM((2, 2, YS // 2, 2, piece, half), BF16),
            pltpu.VMEM((2, 2, YS // 2, 2, piece, half), BF16),
            pltpu.VMEM((2, piece, half), BF16),
            pltpu.VMEM((2, piece, half), BF16),
            pltpu.VMEM((n_col, 1, blocks * share), F32),
            pltpu.VMEM((YS, 1, blocks * share), F32),
            pltpu.VMEM((1, blocks * share), F32),
            pltpu.VMEM((1, blocks * share), F32),
            pltpu.SemaphoreType.DMA((COPIES,)),
            pltpu.SemaphoreType.DMA((COPIES,)),
            pltpu.SemaphoreType.DMA,
        ],
        compiler_params=pltpu.CompilerParams(collective_id=0, has_side_effects=True),
    )(
        jnp.transpose(inputs[0], (1, 2, 0)),
        gain,
        weight,
        cotangent[0],
    )
    anywhere = pl.BlockSpec(memory_space=pl.ANY)
    outputs, input_grad, gain_grad, weight_grad = pl.pallas_call(
        hand_out,
        out_shape=tuple(jax.ShapeDtypeStruct(r.shape, r.dtype) for r in results),
        in_specs=[anywhere] * len(results),
        out_specs=(anywhere,) * len(results),
        scratch_shapes=[pltpu.VMEM(r.shape, r.dtype) for r in results]
        + [pltpu.SemaphoreType.DMA((len(results),)), pltpu.SemaphoreType.DMA((len(results),))],
    )(*results)
    return (
        outputs[None],
        jnp.transpose(input_grad, (2, 0, 1))[None],
        gain_grad,
        weight_grad[None],
    )


def solution(mesh):
    return jax.shard_map(
        body,
        mesh=mesh,
        in_specs=(
            P("dp", "col", None, "row"),
            P(None, "row"),
            P("col", "row"),
            P("dp", "col", "row"),
        ),
        out_specs=(
            P("dp", "col", "row"),
            P("dp", "col", None, "row"),
            P(None, "row"),
            P("col", "dp", "row"),
        ),
        check_vma=False,
    )
```
